32 devices in a mesh: rows: 8 (over y, x, core), cols: 4 (over z).
Axes of the slice: x: 2, y: 2, z: 4, core: 2. Of those that a mesh axis runs over, the one named last changes fastest.
Arguments:
- images: float32 [4, 56, 28, 512], P(None, 'rows', 'cols')
- cotangent: float32 [4, 56, 28, 512], P(None, 'rows', 'cols'), may hold values from -6 to 6
- rel_index: int32 [49, 49], replicated, may hold values from 0 to 168, as said below
- rel_table: float32 [169, 16], replicated
- qkv_weight: bfloat16 [512, 1536], P(('rows', 'cols')), may hold values from -0.25 to 0.25
- proj_weight: bfloat16 [512, 512], P(('rows', 'cols')), may hold values from -1 to 1
- up_weight: bfloat16 [512, 2048], P(('rows', 'cols')), may hold values from -0.25 to 0.25
- down_weight: bfloat16 [2048, 512], P(('rows', 'cols')), may hold values from -0.125 to 0.125
- norm1_gain: bfloat16 [512], P(('rows', 'cols')), may hold values from 0.5 to 1.5
- norm1_bias: bfloat16 [512], P(('rows', 'cols')), may hold values from -3 to 3
- query_bias: bfloat16 [512], P(('rows', 'cols')), may hold values from -3 to 3
- value_bias: bfloat16 [512], P(('rows', 'cols')), may hold values from -3 to 3
- proj_bias: bfloat16 [512], P(('rows', 'cols')), may hold values from -3 to 3
- norm2_gain: bfloat16 [512], P(('rows', 'cols')), may hold values from 0.5 to 1.5
- norm2_bias: bfloat16 [512], P(('rows', 'cols')), may hold values from -3 to 3
- up_bias: bfloat16 [2048], P(('rows', 'cols')), may hold values from -3 to 3
- down_bias: bfloat16 [512], P(('rows', 'cols')), may hold values from -3 to 3
Outputs:
- block_out: float32 [4, 56, 28, 512], P(None, 'rows', 'cols')
- grad_images: float32 [4, 56, 28, 512], P(None, 'rows', 'cols')
- grad_qkv_weight: float32 [512, 1536], P(('rows', 'cols'))
- grad_proj_weight: float32 [512, 512], P(('rows', 'cols'))
- grad_up_weight: float32 [512, 2048], P(('rows', 'cols'))
- grad_down_weight: float32 [2048, 512], P(('rows', 'cols'))
- grad_norm1_gain: float32 [512], P(('rows', 'cols'))
- grad_norm1_bias: float32 [512], P(('rows', 'cols'))
- grad_query_bias: float32 [512], P(('rows', 'cols'))
- grad_value_bias: float32 [512], P(('rows', 'cols'))
- grad_proj_bias: float32 [512], P(('rows', 'cols'))
- grad_norm2_gain: float32 [512], P(('rows', 'cols'))
- grad_norm2_bias: float32 [512], P(('rows', 'cols'))
- grad_up_bias: float32 [2048], P(('rows', 'cols'))
- grad_down_bias: float32 [512], P(('rows', 'cols'))
- grad_rel_table: float32 [169, 16], replicated
The draws below stay inside these ranges and needn't reach their ends.
Inputs may be any that keep to these rules, and one draw needn't show every extreme that they name: `rel_index`: every value from 0 to 168 appears.
All inputs are finite; a program needn't handle non-finite values.
Results may differ from the reference program's by a relative error of at most 0.012.
Values may be sent and summed in bfloat16 or wider, within the bound.
A program may use at most 128 MiB of HBM per device.

```python
import math
import jax
import jax.numpy as jnp
from jax import lax

D = 512
FF = 2048
HEADS = 16
WIN = 7
IMAGES = 4
SHIFT = 3
REL = 169
NH = 56
NW = 28
N_ROWS = 8
N_COLS = 4


def draw_images(key, part):
    key_vals, key_cols, key_rows = jax.random.split(key, 3)
    shape = (IMAGES, NH, NW, D)
    col_scale = jnp.exp(jax.random.uniform(key_cols, (D,), minval=math.log(0.3), maxval=math.log(3.0)))
    row_scale = jnp.exp(jax.random.uniform(key_rows, (IMAGES, NH, NW, 1), minval=math.log(0.3), maxval=math.log(3.0)))
    values = jax.random.normal(key_vals, shape) * col_scale * row_scale
    return values.astype(jnp.float32)


def draw_rel_index(key, part):
    key_fill, key_head, key_order = jax.random.split(jax.random.fold_in(key, 11), 3)
    window = WIN * WIN
    filler = jax.random.randint(key_fill, (window * window - REL,), 0, REL).astype(jnp.int32)
    leading = jax.random.permutation(key_head, REL).astype(jnp.int32)
    joined = jnp.concatenate([leading, filler])
    order = jax.random.permutation(key_order, window * window)
    return joined[order].reshape(window, window).astype(jnp.int32)


def draw_rel_table(key, part):
    key_base = jax.random.fold_in(jax.random.fold_in(key, 23), 0)
    values = jax.random.normal(key_base, (REL, HEADS))
    return values.astype(jnp.float32)


def steps_of(key, shape, pieces, smallest, top_value):
    loudness = 1.0
    for dim, blocks in pieces:
        steps = jax.random.uniform(jax.random.fold_in(jax.random.fold_in(key, 6), dim), (blocks,), jnp.float32, smallest / len(pieces), top_value / len(pieces))
        loudness = loudness * jnp.repeat(jnp.exp(steps), shape[dim] // blocks).reshape((-1,) + (1,) * (len(shape) - 1 - dim))
    return loudness


def bell_draw(own_key, extent, deviation, bound, pieces=(), held_as=jnp.bfloat16):
    values = jax.random.normal(own_key, extent, jnp.float32) * deviation
    if len(pieces) > 0:
        values = steps_of(own_key, extent, pieces, -0.22, 0.18) * values
    return jnp.clip(values, min=-bound, max=bound).astype(held_as)


def setup_inputs(seed: int = 0) -> dict:
    key_of = jax.random.split(jax.random.key(seed), 18)
    return {
        "images": draw_images(jax.random.fold_in(key_of[17], 71), 0),
        "cotangent": bell_draw(key_of[1], (IMAGES, NH, NW, D), 1.0, 6.0, ((1, 8), (2, 4)), jnp.float32),
        "rel_index": draw_rel_index(jax.random.fold_in(key_of[17], 71), 0),
        "rel_table": draw_rel_table(jax.random.fold_in(key_of[17], 71), 0),
        "qkv_weight": bell_draw(key_of[4], (D, 3 * D), D ** -0.5, 0.25, ((0, 32),)),
        "proj_weight": bell_draw(key_of[5], (D, D), (D // 16) ** -0.5, 1.0, ((0, 32),)),
        "up_weight": bell_draw(key_of[6], (D, FF), D ** -0.5, 0.25, ((0, 32),)),
        "down_weight": bell_draw(key_of[7], (FF, D), FF ** -0.5, 0.125, ((0, 32),)),
        "norm1_gain": jnp.clip(1.0 + 0.1 * jax.random.normal(key_of[8], (D,), jnp.float32), 0.5, 1.5).astype(jnp.bfloat16),
        "norm1_bias": bell_draw(key_of[9], (D,), 0.5, 3.0, ((0, 32),)),
        "query_bias": bell_draw(key_of[10], (D,), 0.5, 3.0, ((0, 32),)),
        "value_bias": bell_draw(key_of[11], (D,), 0.5, 3.0, ((0, 32),)),
        "proj_bias": bell_draw(key_of[12], (D,), 0.5, 3.0, ((0, 32),)),
        "norm2_gain": jnp.clip(1.0 + 0.1 * jax.random.normal(key_of[13], (D,), jnp.float32), 0.5, 1.5).astype(jnp.bfloat16),
        "norm2_bias": bell_draw(key_of[14], (D,), 0.5, 3.0, ((0, 32),)),
        "up_bias": bell_draw(key_of[15], (FF,), 0.5, 3.0, ((0, 32),)),
        "down_bias": bell_draw(key_of[16], (D,), 0.5, 3.0, ((0, 32),)),
    }


norm_eps = 1e-05
root_half = 0.7071067811865476
tau_factor = 0.3989422804014327
big_negative = -1e+30

def layer_norm(values, gain_vec, offset):
    mean_val = lax.optimization_barrier(jnp.mean(values, axis=-1, keepdims=True))
    centred = values - mean_val
    inv_std = lax.rsqrt(lax.optimization_barrier(jnp.mean(centred * centred, axis=-1, keepdims=True)) + norm_eps)
    normed = centred * inv_std
    return (normed * gain_vec + offset, normed, inv_std)

def norm_back(grad_out, normed, inv_std, gain_vec):
    scaled = grad_out * gain_vec
    row_inner = scaled - lax.optimization_barrier(jnp.mean(scaled, axis=-1, keepdims=True)) - normed * lax.optimization_barrier(jnp.mean(scaled * normed, axis=-1, keepdims=True))
    return (inv_std * row_inner, lax.optimization_barrier(jnp.sum(grad_out * normed, axis=0)), lax.optimization_barrier(jnp.sum(grad_out, axis=0)))

def dot_plain(former, latter):
    return jnp.dot(former, latter, preferred_element_type=jnp.float32)

def dot_lead(former, latter):
    return lax.dot_general(former, latter, (((0,), (0,)), ((), ())), preferred_element_type=jnp.float32)

def dot_tail(former, latter):
    return lax.dot_general(former, latter, (((1,), (1,)), ((), ())), preferred_element_type=jnp.float32)

def band_of(positions, length):
    return (positions >= length - WIN).astype(jnp.int32) + (positions >= length - SHIFT).astype(jnp.int32)

def window_pass(tokens, grad_rows, allowed, bias_heads, params):
    qkv_weight, proj_weight, up_weight, down_weight, norm1_gain, norm1_bias, query_bias, value_bias, proj_bias, norm2_gain, norm2_bias, up_bias, down_bias = params
    row_total, features = tokens.shape
    window = allowed.shape[-1]
    image_windows = row_total // window
    head_count = bias_heads.shape[0]
    head_width = features // head_count
    score_scale = head_width ** (-0.5)
    highest = lax.Precision.HIGHEST

    def split_heads(values):
        return values.astype(jnp.float32).reshape(image_windows, window, head_count, head_width)

    def scores_of(query_b, key_b):
        raw_scores = jnp.einsum('wqhd,wkhd->whqk', split_heads(query_b), split_heads(key_b), precision=highest)
        return jnp.where(allowed, raw_scores + bias_heads[None], big_negative)
    gain_one = norm1_gain.astype(jnp.float32)
    gain_two = norm2_gain.astype(jnp.float32)
    out_one, normed_one, inv_one = layer_norm(tokens, gain_one, norm1_bias.astype(jnp.float32))
    h_one = out_one.astype(jnp.bfloat16)
    projected = dot_plain(h_one, qkv_weight)
    query_b = ((projected[:, :features] + query_bias.astype(jnp.float32)) * score_scale).astype(jnp.bfloat16)
    key_b = projected[:, features:2 * features].astype(jnp.bfloat16)
    value_b = (projected[:, 2 * features:] + value_bias.astype(jnp.float32)).astype(jnp.bfloat16)
    scores = scores_of(query_b, key_b)
    row_top = lax.optimization_barrier(jnp.max(scores, axis=-1, keepdims=True))
    log_total = row_top + jnp.log(lax.optimization_barrier(jnp.sum(jnp.exp(scores - row_top), axis=-1, keepdims=True)))
    attend_b = jnp.exp(scores - log_total).astype(jnp.bfloat16)
    attn_b = jnp.einsum('whqk,wkhd->wqhd', attend_b.astype(jnp.float32), split_heads(value_b), precision=highest).reshape(row_total, features).astype(jnp.bfloat16)
    residual = tokens + dot_plain(attn_b, proj_weight) + proj_bias.astype(jnp.float32)
    out_two, normed_two, inv_two = layer_norm(residual, gain_two, norm2_bias.astype(jnp.float32))
    h_two = out_two.astype(jnp.bfloat16)
    hidden_pre = dot_plain(h_two, up_weight) + up_bias.astype(jnp.float32)
    gauss_cdf = 0.5 * (1.0 + lax.erf(hidden_pre * root_half))
    act_b = (hidden_pre * gauss_cdf).astype(jnp.bfloat16)
    result = residual + dot_plain(act_b, down_weight) + down_bias.astype(jnp.float32)
    grad_b = grad_rows.astype(jnp.bfloat16)
    grad_down = dot_lead(act_b, grad_b)
    grad_down_add = lax.optimization_barrier(jnp.sum(grad_rows, axis=0))
    grad_act = dot_tail(grad_b, down_weight)
    density = jnp.exp(-0.5 * hidden_pre * hidden_pre) * tau_factor
    grad_pre = grad_act * (gauss_cdf + hidden_pre * density)
    grad_pre_b = grad_pre.astype(jnp.bfloat16)
    grad_up = dot_lead(h_two, grad_pre_b)
    grad_up_add = lax.optimization_barrier(jnp.sum(grad_pre, axis=0))
    grad_h_two = dot_tail(grad_pre_b, up_weight)
    grad_resid, grad_gain_two, grad_bias_two = norm_back(grad_h_two, normed_two, inv_two, gain_two)
    grad_resid = grad_resid + grad_rows
    grad_resid_b = grad_resid.astype(jnp.bfloat16)
    grad_proj = dot_lead(attn_b, grad_resid_b)
    grad_proj_add = lax.optimization_barrier(jnp.sum(grad_resid, axis=0))
    grad_attn_b = dot_tail(grad_resid_b, proj_weight).astype(jnp.bfloat16)
    grad_heads = split_heads(grad_attn_b)
    grad_attend = jnp.einsum('wqhd,wkhd->whqk', grad_heads, split_heads(value_b), precision=highest)
    attend = jnp.exp(scores_of(query_b, key_b) - log_total)
    grad_value = jnp.einsum('whqk,wqhd->wkhd', attend.astype(jnp.bfloat16).astype(jnp.float32), grad_heads, precision=highest).reshape(row_total, features)
    row_inner = lax.optimization_barrier(jnp.sum(attend * grad_attend, axis=-1, keepdims=True))
    grad_scores = attend * (grad_attend - row_inner)
    grad_bias_heads = lax.optimization_barrier(jnp.sum(grad_scores, axis=0)).reshape(head_count, window * window)
    grad_scores_b = grad_scores.astype(jnp.bfloat16)
    grad_query = (jnp.einsum('whqk,wkhd->wqhd', grad_scores_b.astype(jnp.float32), split_heads(key_b), precision=highest) * score_scale).reshape(row_total, features)
    grad_key = jnp.einsum('whqk,wqhd->wkhd', grad_scores_b.astype(jnp.float32), split_heads(query_b), precision=highest).reshape(row_total, features)
    grad_query_add = lax.optimization_barrier(jnp.sum(grad_query, axis=0))
    grad_value_add = lax.optimization_barrier(jnp.sum(grad_value, axis=0))
    grad_mixed_b = jnp.concatenate([grad_query, grad_key, grad_value], axis=1).astype(jnp.bfloat16)
    grad_qkv = dot_lead(h_one, grad_mixed_b)
    grad_h_one = dot_tail(grad_mixed_b, qkv_weight)
    grad_in, grad_gain_one, grad_bias_one = norm_back(grad_h_one, normed_one, inv_one, gain_one)
    grad_tokens = grad_resid + grad_in
    grads = (grad_qkv, grad_proj, grad_up, grad_down, grad_gain_one, grad_bias_one, grad_query_add, grad_value_add, grad_proj_add, grad_gain_two, grad_bias_two, grad_up_add, grad_down_add)
    return (result, grad_tokens, grads, grad_bias_heads)

def to_windows(grid_vals):
    channels = grid_vals.shape[-1]
    return grid_vals.reshape(N_ROWS, WIN, N_COLS, WIN, channels).transpose(0, 2, 1, 3, 4).reshape(N_ROWS * N_COLS, WIN * WIN, channels)

def from_windows(windows):
    channels = windows.shape[-1]
    return windows.reshape(N_ROWS, N_COLS, WIN, WIN, channels).transpose(0, 2, 1, 3, 4).reshape(NH, NW, channels)

def reference(images, cotangent, rel_index, rel_table, qkv_weight, proj_weight, up_weight, down_weight, norm1_gain, norm1_bias, query_bias, value_bias, proj_bias, norm2_gain, norm2_bias, up_bias, down_bias):
    params = (qkv_weight, proj_weight, up_weight, down_weight, norm1_gain, norm1_bias, query_bias, value_bias, proj_bias, norm2_gain, norm2_bias, up_bias, down_bias)
    window = WIN * WIN
    onehot = (rel_index.reshape(window * window).astype(jnp.int32)[:, None] == jnp.arange(REL, dtype=jnp.int32)[None, :]).astype(jnp.float32)
    bias_flat = jnp.dot(onehot, rel_table, precision=lax.Precision.HIGHEST, preferred_element_type=jnp.float32)
    bias_heads = bias_flat.T.reshape(HEADS, window, window)
    band_rows = band_of(jnp.arange(NH, dtype=jnp.int32), NH)
    band_cols = band_of(jnp.arange(NW, dtype=jnp.int32), NW)
    region_grid = 3 * band_rows[:, None] + band_cols[None, :]
    region_win = to_windows(region_grid[:, :, None])[:, :, 0]
    allowed = (region_win[:, :, None] == region_win[:, None, :])[:, None]

    def per_image(totals, image_pair):
        image, grad_image = image_pair
        rolled = jnp.roll(image, (-SHIFT, -SHIFT), axis=(0, 1))
        rolled_grad = jnp.roll(grad_image, (-SHIFT, -SHIFT), axis=(0, 1))
        tokens = to_windows(rolled).reshape(-1, D)
        grad_rows = to_windows(rolled_grad).reshape(-1, D)
        result, grad_tokens, grads, grad_bias = window_pass(tokens, grad_rows, allowed, bias_heads, params)
        totals = jax.tree.map(jnp.add, totals, grads + (grad_bias,))
        out_image = jnp.roll(from_windows(result.reshape(-1, window, D)), (SHIFT, SHIFT), axis=(0, 1))
        grad_out_image = jnp.roll(from_windows(grad_tokens.reshape(-1, window, D)), (SHIFT, SHIFT), axis=(0, 1))
        return (totals, (out_image, grad_out_image))
    zeros_init = tuple((jnp.zeros(p.shape, jnp.float32) for p in params)) + (jnp.zeros((HEADS, window * window), jnp.float32),)
    totals_end, (block_out, grad_images) = lax.scan(per_image, zeros_init, (images, cotangent))
    grad_rel_table = lax.dot_general(onehot, totals_end[13], (((0,), (1,)), ((), ())), precision=lax.Precision.HIGHEST, preferred_element_type=jnp.float32)
    return (block_out, grad_images, totals_end[0], totals_end[1], totals_end[2], totals_end[3], totals_end[4], totals_end[5], totals_end[6], totals_end[7], totals_end[8], totals_end[9], totals_end[10], totals_end[11], totals_end[12], grad_rel_table)
```

```python
import functools

import jax
import jax.numpy as jnp
from jax import lax
from jax.experimental import pallas as pl
from jax.experimental.pallas import tpu as pltpu
from jax.sharding import PartitionSpec as P

WIN = 7
SHIFT = 3


norm_eps = 1e-05
root_half = 0.7071067811865476
tau_factor = 0.3989422804014327
big_negative = -1e30


def shifted(array, axis, by):
    length = lax.axis_size(axis)
    return lax.ppermute(array, axis, [(i, (i + by) % length) for i in range(length)])


def as_sent(array):

    def short(part):
        return part.astype(jnp.bfloat16) if part.dtype == jnp.float32 else part

    return jax.tree.map(short, array)


def layer_norm(values, gain_vec, offset):
    mean_val = jnp.mean(values, axis=-1, keepdims=True)
    centred = values - mean_val
    inv_std = lax.rsqrt(jnp.mean(centred * centred, axis=-1, keepdims=True) + norm_eps)
    normed = centred * inv_std
    return (normed * gain_vec + offset, normed, inv_std)


def norm_back(grad_out, normed, inv_std, gain_vec):
    scaled = grad_out * gain_vec
    row_inner = (
        scaled
        - jnp.mean(scaled, axis=-1, keepdims=True)
        - normed * jnp.mean(scaled * normed, axis=-1, keepdims=True)
    )
    return (inv_std * row_inner, jnp.sum(grad_out * normed, axis=0), jnp.sum(grad_out, axis=0))


def dot_plain(former, latter):
    return jnp.dot(former, latter, preferred_element_type=jnp.float32)


def dot_lead(former, latter):
    return lax.dot_general(
        former, latter, (((0,), (0,)), ((), ())), preferred_element_type=jnp.float32
    )


def dot_tail(former, latter):
    return lax.dot_general(
        former, latter, (((1,), (1,)), ((), ())), preferred_element_type=jnp.float32
    )


def band_of(positions, length):
    return (positions >= length - WIN).astype(jnp.int32) + (positions >= length - SHIFT).astype(
        jnp.int32
    )


def roll_in(images, cotangent):
    from_below = shifted((images[:, :SHIFT], cotangent[:, :SHIFT]), "rows", -1)
    tall_tokens = jnp.concatenate([images[:, SHIFT:], from_below[0]], axis=1)
    tall_grads = jnp.concatenate([cotangent[:, SHIFT:], from_below[1]], axis=1)
    beside = shifted((tall_tokens[:, :, :SHIFT], tall_grads[:, :, :SHIFT]), "cols", -1)
    return (
        jnp.concatenate([tall_tokens[:, :, SHIFT:], beside[0]], axis=2),
        jnp.concatenate([tall_grads[:, :, SHIFT:], beside[1]], axis=2),
    )


def roll_out(result, grad_tokens):
    from_above = (
        shifted(result[:, -SHIFT:].astype(jnp.bfloat16), "rows", 1).astype(jnp.float32),
        shifted(grad_tokens[:, -SHIFT:].astype(jnp.bfloat16), "rows", 1).astype(jnp.float32),
    )
    tall_result = jnp.concatenate([from_above[0], result[:, :-SHIFT]], axis=1)
    tall_grads = jnp.concatenate([from_above[1], grad_tokens[:, :-SHIFT]], axis=1)
    beside = (
        shifted(tall_result[:, :, -SHIFT:].astype(jnp.bfloat16), "cols", 1).astype(jnp.float32),
        shifted(as_sent(tall_grads[:, :, -SHIFT:]), "cols", 1),
    )
    return (
        jnp.concatenate([beside[0], tall_result[:, :, :-SHIFT]], axis=2),
        jnp.concatenate([beside[1], tall_grads[:, :, :-SHIFT]], axis=2),
    )


MESH = pl.DeviceIdType.MESH
CORES = 2


def grid_of(rows):
    chips = rows // CORES
    across = 1
    for size in range(1, chips + 1):
        if chips % size == 0 and size * size <= chips:
            across = size
    return chips // across, across


def whereabouts(dims):
    height, width = dims[0], dims[1]
    row, depth_at = lax.axis_index("rows"), lax.axis_index("cols")
    core = lax.rem(row, CORES)
    chip = row // CORES
    return chip // width, lax.rem(chip, width), core, depth_at


def device_at(dims, y, x, core, z):
    return ((y * dims[1] + x) * CORES + core, z)


def greet(dims, here):
    barrier = pltpu.get_barrier_semaphore()
    total = 0
    for axis in range(4):
        for step in range(1, dims[axis]):
            there = list(here)
            there[axis] = lax.rem(here[axis] + step, dims[axis])
            pl.semaphore_signal(
                barrier, inc=1, device_id=device_at(dims, *there), device_id_type=MESH
            )
            total += 1
    pl.semaphore_wait(barrier, total)


def moved(here, axis, step, dims):
    there = list(here)
    there[axis] = lax.rem(here[axis] + step, dims[axis])
    return there


def gather_kernel(dims, count, *refs):
    ins, outs = refs[:count], refs[count : 2 * count]
    local_sem, send_sem, recv_sem = refs[2 * count :]
    height, width, _, depth = dims
    here = whereabouts(dims)
    y, x, core, z = here
    greet(dims, here)
    used = [0] * count

    def send(stream, src, dst, there):
        slot = used[stream]
        used[stream] += 1
        copy = pltpu.make_async_remote_copy(
            src_ref=src,
            dst_ref=dst,
            send_sem=send_sem.at[stream, slot],
            recv_sem=recv_sem.at[stream, slot],
            device_id=device_at(dims, *there),
            device_id_type=MESH,
        )
        copy.start()
        return copy

    started = []
    along_z, locals_ = [], []
    for k in range(count):
        mine = pltpu.make_async_copy(ins[k], outs[k].at[y, x, core, z], local_sem.at[k])
        mine.start()
        locals_.append(mine)
        along_z.append(
            [
                send(k, ins[k], outs[k].at[y, x, core, z], moved(here, 3, step, dims))
                for step in range(1, depth)
            ]
        )
        started += along_z[k]
    first, second, partner = [], [], []
    other = moved(here, 2, 1, dims)
    for k in range(count):
        locals_[k].wait()
        for copy in along_z[k]:
            copy.wait_recv()
        axis = k % 2
        block = outs[k].at[y, x, core]
        first.append(
            [send(k, block, block, moved(here, axis, s, dims)) for s in range(1, dims[axis])]
        )
        partner.append([send(k, block, block, other)])
        started += first[k] + partner[k]
    for k in range(count):
        axis = k % 2
        cross = 1 - axis
        for copy in first[k]:
            copy.wait_recv()
        copies = []
        for lag in range(dims[axis]):
            at = moved(here, axis, lag, dims)
            block = outs[k].at[at[0], at[1], core]
            copies += [
                send(k, block, block, moved(here, cross, s, dims)) for s in range(1, dims[cross])
            ]
            if lag:
                partner[k].append(send(k, block, block, other))
                started.append(partner[k][-1])
        second.append(copies)
        started += copies
    for k in range(count):
        axis = k % 2
        cross = 1 - axis
        copies = iter(second[k])
        for lag in range(dims[axis]):
            for s in range(1, dims[cross]):
                next(copies).wait_recv()
                at = moved(here, axis, lag, dims)
                at[cross] = lax.rem(here[cross] + dims[cross] - s, dims[cross])
                block = outs[k].at[at[0], at[1], core]
                partner[k].append(send(k, block, block, other))
                started.append(partner[k][-1])
    for k in range(count):
        for copy in partner[k]:
            copy.wait_recv()
    for copy in started:
        copy.wait_send()


def reduce_kernel(dims, count, *refs):
    ins, table = refs[:count], refs[count]
    outs, table_out = refs[count + 1 : 2 * count + 1], refs[2 * count + 1]
    rest = refs[2 * count + 2 :]
    bufs = [rest[7 * k : 7 * k + 7] for k in range(count)]
    table_in = rest[7 * count : 7 * count + 4]
    table_sum = rest[7 * count + 4 : 7 * count + 7]
    send_sem, recv_sem = rest[7 * count + 7 :]
    height, width, _, depth = dims
    here = whereabouts(dims)
    y, x, core, z = here
    greet(dims, here)
    used = [0] * (count + 1)
    started = []

    def send(stream, src, dst, there):
        slot = used[stream]
        used[stream] += 1
        copy = pltpu.make_async_remote_copy(
            src_ref=src,
            dst_ref=dst,
            send_sem=send_sem.at[stream, slot],
            recv_sem=recv_sem.at[stream, slot],
            device_id=device_at(dims, *there),
            device_id_type=MESH,
        )
        copy.start()
        started.append(copy)
        return copy

    def add(dst, parts):
        def body(i, carry):
            total = parts[0][i].astype(jnp.float32)
            for part in parts[1:]:
                total = total + part[i].astype(jnp.float32)
            dst[i] = total.astype(dst.dtype)
            return carry

        lax.fori_loop(0, depth, body, 0)

    def table_step(stage, axis, src):
        table_in[stage][here[axis]] = src[...]
        return [
            send(count, src, table_in[stage].at[here[axis]], moved(here, axis, s, dims))
            for s in range(1, dims[axis])
        ]

    def table_add(stage, axis, copies, dst):
        for copy in copies:
            copy.wait_recv()
        total = table_in[stage][0]
        for j in range(1, dims[axis]):
            total = total + table_in[stage][j]
        dst[...] = total

    other = moved(here, 2, 1, dims)
    table_copies = table_step(0, 2, table)
    core_copies = []
    for k in range(count):
        axis = k % 2
        cross = 1 - axis
        group = {}
        for lag in list(range(1, dims[axis])) + [0]:
            for j in range(dims[cross]):
                at = moved(here, axis, lag, dims)
                at[cross] = j
                group[lag, j] = send(
                    k, ins[k].at[at[0], at[1], other[2]], bufs[k][0].at[at[0], at[1]], other
                )
        core_copies.append(group)
    table_add(0, 2, table_copies, table_sum[0])
    table_copies = table_step(1, 0, table_sum[0])
    first = []
    for k in range(count):
        axis = k % 2
        cross = 1 - axis
        from_core, sum_core, from_first = bufs[k][0], bufs[k][1], bufs[k][2]
        group = []
        for lag in list(range(1, dims[axis])) + [0]:
            for j in range(dims[cross]):
                at = moved(here, axis, lag, dims)
                at[cross] = j
                core_copies[k][lag, j].wait_recv()
                block = sum_core.at[at[0], at[1]]
                add(block, [ins[k].at[at[0], at[1], core], from_core.at[at[0], at[1]]])
                if lag:
                    group.append(
                        send(k, block, from_first.at[lag - 1, j], moved(here, axis, lag, dims))
                    )
        first.append(group)
    table_add(1, 0, table_copies, table_sum[1])
    table_copies = table_step(2, 1, table_sum[1])
    second = []
    for k in range(count):
        axis = k % 2
        cross = 1 - axis
        sum_core, from_first, sum_first, from_second = bufs[k][1:5]
        for copy in first[k]:
            copy.wait_recv()
        group = []
        for lag in list(range(1, dims[cross])) + [0]:
            at = moved(here, cross, lag, dims)
            j = at[cross]
            block = sum_first.at[j]
            add(
                block,
                [sum_core.at[at[0], at[1]]]
                + [from_first.at[s - 1, j] for s in range(1, dims[axis])],
            )
            if lag:
                group.append(send(k, block, from_second.at[lag - 1], at))
        second.append(group)
    table_add(2, 1, table_copies, table_sum[2])
    table_copies = table_step(3, 3, table_sum[2])
    third = []
    for k in range(count):
        axis = k % 2
        cross = 1 - axis
        sum_first, from_second, sum_second, from_third = bufs[k][3:7]
        for copy in second[k]:
            copy.wait_recv()
        add(
            sum_second,
            [sum_first.at[here[cross]]] + [from_second.at[s - 1] for s in range(1, dims[cross])],
        )
        group = []
        for step in range(1, depth):
            at = moved(here, 3, step, dims)
            group.append(send(k, sum_second.at[at[3]], from_third.at[step - 1], at))
        third.append(group)
    table_add(3, 3, table_copies, table_out)
    for k in range(count):
        sum_second, from_third = bufs[k][5:7]
        for copy in third[k]:
            copy.wait_recv()
        total = sum_second[z].astype(jnp.float32)
        for step in range(1, depth):
            total = total + from_third[step - 1].astype(jnp.float32)
        outs[k][...] = total
    for copy in started:
        copy.wait_send()


def sizes_here():
    rows, depth = lax.axis_size("rows"), lax.axis_size("cols")
    height, width = grid_of(rows)
    return height, width, CORES, depth


def blocked(rows, columns):
    if rows % 16 == 0:
        return rows, columns
    return rows * columns // 128, 128


def gather_all(shards):
    dims = sizes_here()
    height, width, cores, depth = dims
    count = len(shards)
    blocks = [blocked(*shard.shape) for shard in shards]
    slots = (depth - 1) + max(height, width) * 2 * height * width
    outs = pl.pallas_call(
        functools.partial(gather_kernel, dims, count),
        name="gather_all",
        out_shape=[
            jax.ShapeDtypeStruct(dims + block, shard.dtype)
            for block, shard in zip(blocks, shards)
        ],
        in_specs=[pl.BlockSpec(memory_space=pltpu.VMEM)] * count,
        out_specs=[pl.BlockSpec(memory_space=pl.ANY)] * count,
        scratch_shapes=[
            pltpu.SemaphoreType.DMA((count,)),
            pltpu.SemaphoreType.DMA((count, slots)),
            pltpu.SemaphoreType.DMA((count, slots)),
        ],
        compiler_params=pltpu.CompilerParams(collective_id=0, has_side_effects=True),
    )(*[shard.reshape(block) for block, shard in zip(blocks, shards)])
    total = height * width * cores * depth
    return [
        out.reshape(total * shard.shape[0], shard.shape[1]) for out, shard in zip(outs, shards)
    ]


def reduce_all(wholes, table):
    dims = sizes_here()
    height, width, cores, depth = dims
    total = height * width * cores * depth
    count = len(wholes)
    shares = [(whole.shape[0] // total, whole.shape[1]) for whole in wholes]
    blocks = [blocked(*share) for share in shares]
    scratch = []
    for k, (block, whole) in enumerate(zip(blocks, wholes)):
        along, cross = dims[k % 2], dims[1 - k % 2]
        for lead in (
            (height, width, depth),
            (height, width, depth),
            (max(along - 1, 1), cross, depth),
            (cross, depth),
            (max(cross - 1, 1), depth),
            (depth,),
            (max(depth - 1, 1),),
        ):
            scratch.append(pltpu.VMEM(lead + block, whole.dtype))
    for size in (cores, height, width, depth):
        scratch.append(pltpu.VMEM((size,) + table.shape, table.dtype))
    scratch += [pltpu.VMEM(table.shape, table.dtype)] * 3
    slots = 2 * height * width + height + width + depth
    scratch += [pltpu.SemaphoreType.DMA((count + 1, slots))] * 2
    outs = pl.pallas_call(
        functools.partial(reduce_kernel, dims, count),
        name="reduce_all",
        out_shape=[jax.ShapeDtypeStruct(block, jnp.float32) for block in blocks]
        + [jax.ShapeDtypeStruct(table.shape, table.dtype)],
        in_specs=[pl.BlockSpec(memory_space=pltpu.VMEM)] * (count + 1),
        out_specs=[pl.BlockSpec(memory_space=pltpu.VMEM)] * (count + 1),
        scratch_shapes=scratch,
        compiler_params=pltpu.CompilerParams(collective_id=1, has_side_effects=True),
    )(*[whole.reshape(dims + block) for block, whole in zip(blocks, wholes)], table)
    return [out.reshape(share) for out, share in zip(outs, shares)], outs[-1]


def padded(values, multiple):
    size = values.shape[-1]
    extra = -size % multiple
    return jnp.pad(values, [(0, 0)] * (values.ndim - 1) + [(0, extra)])


def per_device(
    images,
    cotangent,
    rel_index,
    rel_table,
    qkv_weight,
    proj_weight,
    up_weight,
    down_weight,
    norm1_gain,
    norm1_bias,
    query_bias,
    value_bias,
    proj_bias,
    norm2_gain,
    norm2_bias,
    up_bias,
    down_bias,
):
    shards = (
        norm1_gain,
        norm1_bias,
        query_bias,
        value_bias,
        proj_bias,
        norm2_gain,
        norm2_bias,
        up_bias,
        down_bias,
    )
    vector_shard = padded(jnp.concatenate(shards)[None], 2048).reshape(-1, 128)
    qkv_full, down_full, up_full, proj_full, vector_full = gather_all(
        [qkv_weight, down_weight, up_weight, proj_weight, vector_shard]
    )
    device_count = lax.axis_size("rows") * lax.axis_size("cols")
    vector_full = vector_full.reshape(device_count, -1)
    vectors, offset = [], 0
    for shard in shards:
        size = shard.shape[0]
        vectors.append(vector_full[:, offset : offset + size].reshape(device_count * size))
        offset += size
    (
        gain_one_full,
        bias_one_full,
        query_add,
        value_add,
        proj_add,
        gain_two_full,
        bias_two_full,
        up_add,
        down_add,
    ) = vectors
    tokens_tile, grad_tile = roll_in(images, cotangent)
    image_count, tile_side, features = (
        tokens_tile.shape[0],
        tokens_tile.shape[1],
        tokens_tile.shape[3],
    )
    window = tile_side * tile_side
    row_total = image_count * window
    tokens = tokens_tile.reshape(row_total, features)
    grad_rows = grad_tile.reshape(row_total, features)
    local_pos = jnp.arange(tile_side, dtype=jnp.int32)
    band_rows = band_of(
        lax.axis_index("rows") * tile_side + local_pos, lax.axis_size("rows") * tile_side
    )
    band_cols = band_of(
        lax.axis_index("cols") * tile_side + local_pos, lax.axis_size("cols") * tile_side
    )
    region = (3 * band_rows[:, None] + band_cols[None, :]).reshape(window)
    allowed = (region[:, None] == region[None, :])[None, None]
    head_count = rel_table.shape[1]
    table_size = rel_table.shape[0]
    head_width = features // head_count
    score_scale = head_width ** (-0.5)
    onehot = (
        rel_index.reshape(window * window)[:, None]
        == jnp.arange(table_size, dtype=jnp.int32)[None, :]
    ).astype(jnp.float32)
    bias_flat = jnp.dot(
        onehot, rel_table, precision=lax.Precision.HIGHEST, preferred_element_type=jnp.float32
    )
    bias_heads = bias_flat.T.reshape(head_count, window, window)

    def split_heads(values):
        return values.reshape(image_count, window, head_count, head_width)

    def scores_of(query_b, key_b):
        raw_scores = jnp.einsum(
            "wqhd,wkhd->whqk",
            split_heads(query_b),
            split_heads(key_b),
            preferred_element_type=jnp.float32,
        )
        return jnp.where(allowed, raw_scores + bias_heads[None], big_negative)

    gain_one = gain_one_full.astype(jnp.float32)
    gain_two = gain_two_full.astype(jnp.float32)
    out_one, normed_one, inv_one = layer_norm(tokens, gain_one, bias_one_full.astype(jnp.float32))
    h_one = out_one.astype(jnp.bfloat16)
    projected = dot_plain(h_one, qkv_full)
    query_b = ((projected[:, :features] + query_add.astype(jnp.float32)) * score_scale).astype(
        jnp.bfloat16
    )
    key_b = projected[:, features : 2 * features].astype(jnp.bfloat16)
    value_b = (projected[:, 2 * features :] + value_add.astype(jnp.float32)).astype(jnp.bfloat16)
    scores = scores_of(query_b, key_b)
    row_top = jnp.max(scores, axis=-1, keepdims=True)
    log_total = row_top + jnp.log(jnp.sum(jnp.exp(scores - row_top), axis=-1, keepdims=True))
    attend_b = jnp.exp(scores - log_total).astype(jnp.bfloat16)
    attn_b = (
        jnp.einsum(
            "whqk,wkhd->wqhd", attend_b, split_heads(value_b), preferred_element_type=jnp.float32
        )
        .reshape(row_total, features)
        .astype(jnp.bfloat16)
    )
    residual = tokens + dot_plain(attn_b, proj_full) + proj_add.astype(jnp.float32)
    out_two, normed_two, inv_two = layer_norm(residual, gain_two, bias_two_full.astype(jnp.float32))
    h_two = out_two.astype(jnp.bfloat16)
    hidden_pre = dot_plain(h_two, up_full) + up_add.astype(jnp.float32)
    gauss_cdf = 0.5 * (1.0 + lax.erf(hidden_pre * root_half))
    act_b = (hidden_pre * gauss_cdf).astype(jnp.bfloat16)
    result = residual + dot_plain(act_b, down_full) + down_add.astype(jnp.float32)
    grad_b = grad_rows.astype(jnp.bfloat16)
    grad_down = dot_lead(act_b, grad_b)
    grad_down_add = jnp.sum(grad_rows, axis=0)
    grad_act = dot_tail(grad_b, down_full)
    density = jnp.exp(-0.5 * hidden_pre * hidden_pre) * tau_factor
    grad_pre = grad_act * (gauss_cdf + hidden_pre * density)
    grad_pre_b = grad_pre.astype(jnp.bfloat16)
    grad_up = dot_lead(h_two, grad_pre_b)
    grad_up_add = jnp.sum(grad_pre, axis=0)
    grad_h_two = dot_tail(grad_pre_b, up_full)
    grad_resid, grad_gain_two, grad_bias_two = norm_back(
        grad_h_two, normed_two, inv_two, gain_two
    )
    grad_resid = grad_resid + grad_rows
    grad_resid_b = grad_resid.astype(jnp.bfloat16)
    grad_proj = dot_lead(attn_b, grad_resid_b)
    grad_proj_add = jnp.sum(grad_resid, axis=0)
    grad_attn_b = dot_tail(grad_resid_b, proj_full).astype(jnp.bfloat16)
    grad_heads = split_heads(grad_attn_b)
    grad_attend = jnp.einsum(
        "wqhd,wkhd->whqk", grad_heads, split_heads(value_b), preferred_element_type=jnp.float32
    )
    attend = jnp.exp(scores_of(query_b, key_b) - log_total)
    grad_value = jnp.einsum(
        "whqk,wqhd->wkhd",
        attend.astype(jnp.bfloat16),
        grad_heads,
        preferred_element_type=jnp.float32,
    ).reshape(row_total, features)
    row_inner = jnp.sum(attend * grad_attend, axis=-1, keepdims=True)
    grad_scores = attend * (grad_attend - row_inner)
    grad_bias_heads = jnp.sum(grad_scores, axis=0).reshape(head_count, window * window)
    table_local = lax.dot_general(
        onehot,
        grad_bias_heads,
        (((0,), (1,)), ((), ())),
        precision=lax.Precision.HIGHEST,
        preferred_element_type=jnp.float32,
    )
    grad_scores_b = grad_scores.astype(jnp.bfloat16)
    grad_query = (
        jnp.einsum(
            "whqk,wkhd->wqhd", grad_scores_b, split_heads(key_b), preferred_element_type=jnp.float32
        )
        * score_scale
    ).reshape(row_total, features)
    grad_key = jnp.einsum(
        "whqk,wqhd->wkhd", grad_scores_b, split_heads(query_b), preferred_element_type=jnp.float32
    ).reshape(row_total, features)
    grad_query_add = jnp.sum(grad_query, axis=0)
    grad_value_add = jnp.sum(grad_value, axis=0)
    grad_mixed_b = jnp.concatenate([grad_query, grad_key, grad_value], axis=1).astype(jnp.bfloat16)
    grad_qkv = dot_lead(h_one, grad_mixed_b)
    grad_h_one = dot_tail(grad_mixed_b, qkv_full)
    grad_in, grad_gain_one, grad_bias_one = norm_back(
        grad_h_one, normed_one, inv_one, gain_one
    )
    grad_tokens = grad_resid + grad_in
    vector_grads = (
        grad_gain_one,
        grad_bias_one,
        grad_query_add,
        grad_value_add,
        grad_proj_add,
        grad_gain_two,
        grad_bias_two,
        grad_up_add,
        grad_down_add,
    )
    vector_rows = padded(
        jnp.concatenate([grad.reshape(device_count, -1) for grad in vector_grads], axis=1), 2048
    ).reshape(-1, 128)
    table_rows = padded(table_local.reshape(1, -1), 1024).reshape(-1, 128)
    (down_sum, up_sum, qkv_sum, proj_sum, vector_sum), table_sum = reduce_all(
        [
            grad_down.astype(jnp.bfloat16),
            grad_up.astype(jnp.bfloat16),
            grad_qkv.astype(jnp.bfloat16),
            grad_proj.astype(jnp.bfloat16),
            vector_rows,
        ],
        table_rows,
    )
    grad_table = table_sum.reshape(-1)[: table_local.size].reshape(table_local.shape)
    vector_sum = vector_sum.reshape(-1)
    vector_sums, offset = [], 0
    for shard in shards:
        size = shard.shape[0]
        vector_sums.append(vector_sum[offset : offset + size])
        offset += size
    shard_grads = (qkv_sum, proj_sum, up_sum, down_sum, *vector_sums)
    block_out, grad_images = roll_out(
        result.reshape(image_count, tile_side, tile_side, features),
        grad_tokens.reshape(image_count, tile_side, tile_side, features),
    )
    return (
        block_out,
        grad_images,
        shard_grads[0],
        shard_grads[1],
        shard_grads[2],
        shard_grads[3],
        shard_grads[4],
        shard_grads[5],
        shard_grads[6],
        shard_grads[7],
        shard_grads[8],
        shard_grads[9],
        shard_grads[10],
        shard_grads[11],
        shard_grads[12],
        grad_table,
    )


def solution(mesh):
    in_specs = (
        P(None, "rows", "cols", None),
        P(None, "rows", "cols", None),
        P(),
        P(),
        P(("rows", "cols"), None),
        P(("rows", "cols"), None),
        P(("rows", "cols"), None),
        P(("rows", "cols"), None),
        P(("rows", "cols")),
        P(("rows", "cols")),
        P(("rows", "cols")),
        P(("rows", "cols")),
        P(("rows", "cols")),
        P(("rows", "cols")),
        P(("rows", "cols")),
        P(("rows", "cols")),
        P(("rows", "cols")),
    )
    out_specs = (
        P(None, "rows", "cols", None),
        P(None, "rows", "cols", None),
        P(("rows", "cols"), None),
        P(("rows", "cols"), None),
        P(("rows", "cols"), None),
        P(("rows", "cols"), None),
        P(("rows", "cols")),
        P(("rows", "cols")),
        P(("rows", "cols")),
        P(("rows", "cols")),
        P(("rows", "cols")),
        P(("rows", "cols")),
        P(("rows", "cols")),
        P(("rows", "cols")),
        P(("rows", "cols")),
        P(),
    )
    return jax.shard_map(
        per_device, mesh=mesh, in_specs=in_specs, out_specs=out_specs, check_vma=False
    )
```

```python
import functools

import jax
import jax.numpy as jnp
from jax import lax
from jax.experimental import pallas as pl
from jax.experimental.pallas import tpu as pltpu
from jax.sharding import PartitionSpec as P


WIN = 7
SHIFT = 3


norm_eps = 1e-05
root_half = 0.7071067811865476
tau_factor = 0.3989422804014327
big_negative = -1e30


def shifted(array, axis, by):
    length = lax.axis_size(axis)
    return lax.ppermute(array, axis, [(i, (i + by) % length) for i in range(length)])


def layer_norm(values, gain_vec, offset):
    mean_val = jnp.mean(values, axis=-1, keepdims=True)
    centred = values - mean_val
    inv_std = lax.rsqrt(jnp.mean(centred * centred, axis=-1, keepdims=True) + norm_eps)
    normed = centred * inv_std
    return (normed * gain_vec + offset, normed, inv_std)


def norm_back(grad_out, normed, inv_std, gain_vec):
    scaled = grad_out * gain_vec
    row_inner = (
        scaled
        - jnp.mean(scaled, axis=-1, keepdims=True)
        - normed * jnp.mean(scaled * normed, axis=-1, keepdims=True)
    )
    return (inv_std * row_inner, jnp.sum(grad_out * normed, axis=0), jnp.sum(grad_out, axis=0))


def dot_plain(former, latter):
    return jnp.dot(former, latter, preferred_element_type=jnp.float32)


def dot_lead(former, latter):
    return lax.dot_general(
        former, latter, (((0,), (0,)), ((), ())), preferred_element_type=jnp.float32
    )


def dot_tail(former, latter):
    return lax.dot_general(
        former, latter, (((1,), (1,)), ((), ())), preferred_element_type=jnp.float32
    )


def band_of(positions, length):
    return (positions >= length - WIN).astype(jnp.int32) + (positions >= length - SHIFT).astype(
        jnp.int32
    )


def shifted_both(array, by):
    rows, cols = lax.axis_size("rows"), lax.axis_size("cols")
    pairs = [
        (i * cols + j, (i + by) % rows * cols + (j + by) % cols)
        for i in range(rows)
        for j in range(cols)
    ]
    return lax.ppermute(array, ("rows", "cols"), pairs)


def roll_in(both):
    below = shifted(both[:, :SHIFT, SHIFT:], "rows", -1)
    beside = shifted(both[:, SHIFT:, :SHIFT], "cols", -1)
    corner = shifted_both(both[:, :SHIFT, :SHIFT], -1)
    top = jnp.concatenate([both[:, SHIFT:, SHIFT:], beside], axis=2)
    bottom = jnp.concatenate([below, corner], axis=2)
    return jnp.concatenate([top, bottom], axis=1)


def roll_out(values):
    short = values.astype(jnp.bfloat16)
    above = shifted(short[:, -SHIFT:, :-SHIFT], "rows", 1)
    beside = shifted(short[:, :-SHIFT, -SHIFT:], "cols", 1)
    corner = shifted_both(short[:, -SHIFT:, -SHIFT:], 1)
    top = jnp.concatenate([corner, above], axis=2).astype(jnp.float32)
    bottom = jnp.concatenate(
        [beside.astype(jnp.float32), values[:, :-SHIFT, :-SHIFT]], axis=2
    )
    return jnp.concatenate([top, bottom], axis=1)


MESH = pl.DeviceIdType.MESH
CORES = 2


def grid_of(rows):
    chips = rows // CORES
    across = 1
    for size in range(1, chips + 1):
        if chips % size == 0 and size * size <= chips:
            across = size
    return chips // across, across


def whereabouts(dims):
    width = dims[1]
    row, depth_at = lax.axis_index("rows"), lax.axis_index("cols")
    core = lax.rem(row, CORES)
    chip = row // CORES
    return chip // width, lax.rem(chip, width), core, depth_at


def device_at(dims, y, x, core, z):
    return ((y * dims[1] + x) * CORES + core, z)


def greet(dims, here):
    barrier = pltpu.get_barrier_semaphore()
    total = 0
    for axis in range(4):
        for step in range(1, dims[axis]):
            there = list(here)
            there[axis] = lax.rem(here[axis] + step, dims[axis])
            pl.semaphore_signal(
                barrier, inc=1, device_id=device_at(dims, *there), device_id_type=MESH
            )
            total += 1
    pl.semaphore_wait(barrier, total)


def moved(here, axis, step, dims):
    there = list(here)
    there[axis] = lax.rem(here[axis] + step, dims[axis])
    return there


def gather_kernel(dims, count, *refs):
    ins, outs = refs[:count], refs[count : 2 * count]
    local_sem, send_sem, recv_sem = refs[2 * count :]
    _, _, _, depth = dims
    here = whereabouts(dims)
    y, x, core, z = here
    greet(dims, here)
    used = [0] * count

    def send(stream, src, dst, there):
        slot = used[stream]
        used[stream] += 1
        copy = pltpu.make_async_remote_copy(
            src_ref=src,
            dst_ref=dst,
            send_sem=send_sem.at[stream, slot],
            recv_sem=recv_sem.at[stream, slot],
            device_id=device_at(dims, *there),
            device_id_type=MESH,
        )
        copy.start()
        return copy

    started = []
    along_z, locals_ = [], []
    for k in range(count):
        mine = pltpu.make_async_copy(ins[k], outs[k].at[y, x, core, z], local_sem.at[k])
        mine.start()
        locals_.append(mine)
        along_z.append(
            [
                send(k, ins[k], outs[k].at[y, x, core, z], moved(here, 3, step, dims))
                for step in range(1, depth)
            ]
        )
        started += along_z[k]
    first, second, partner = [], [], []
    other = moved(here, 2, 1, dims)
    for k in range(count):
        locals_[k].wait()
        for copy in along_z[k]:
            copy.wait_recv()
        axis = k % 2
        block = outs[k].at[y, x, core]
        first.append(
            [send(k, block, block, moved(here, axis, s, dims)) for s in range(1, dims[axis])]
        )
        partner.append([send(k, block, block, other)])
        started += first[k] + partner[k]
    for k in range(count):
        axis = k % 2
        cross = 1 - axis
        for copy in first[k]:
            copy.wait_recv()
        copies = []
        for lag in range(dims[axis]):
            at = moved(here, axis, lag, dims)
            block = outs[k].at[at[0], at[1], core]
            copies += [
                send(k, block, block, moved(here, cross, s, dims)) for s in range(1, dims[cross])
            ]
            if lag:
                partner[k].append(send(k, block, block, other))
                started.append(partner[k][-1])
        second.append(copies)
        started += copies
    for k in range(count):
        axis = k % 2
        cross = 1 - axis
        copies = iter(second[k])
        for lag in range(dims[axis]):
            for s in range(1, dims[cross]):
                next(copies).wait_recv()
                at = moved(here, axis, lag, dims)
                at[cross] = lax.rem(here[cross] + dims[cross] - s, dims[cross])
                block = outs[k].at[at[0], at[1], core]
                partner[k].append(send(k, block, block, other))
                started.append(partner[k][-1])
    for k in range(count):
        for copy in partner[k]:
            copy.wait_recv()
    for copy in started:
        copy.wait_send()


def reduce_kernel(dims, count, *refs):
    ins, table = refs[:count], refs[count]
    outs, table_out = refs[count + 1 : 2 * count + 1], refs[2 * count + 1]
    rest = refs[2 * count + 2 :]
    bufs = [rest[7 * k : 7 * k + 7] for k in range(count)]
    table_in = rest[7 * count : 7 * count + 4]
    table_sum = rest[7 * count + 4 : 7 * count + 7]
    send_sem, recv_sem = rest[7 * count + 7 :]
    _, _, _, depth = dims
    here = whereabouts(dims)
    _, _, core, z = here
    greet(dims, here)
    used = [0] * (count + 1)
    started = []

    def send(stream, src, dst, there):
        slot = used[stream]
        used[stream] += 1
        copy = pltpu.make_async_remote_copy(
            src_ref=src,
            dst_ref=dst,
            send_sem=send_sem.at[stream, slot],
            recv_sem=recv_sem.at[stream, slot],
            device_id=device_at(dims, *there),
            device_id_type=MESH,
        )
        copy.start()
        started.append(copy)
        return copy

    def add(dst, parts):
        def body(i, carry):
            total = parts[0][i].astype(jnp.float32)
            for part in parts[1:]:
                total = total + part[i].astype(jnp.float32)
            dst[i] = total.astype(dst.dtype)
            return carry

        lax.fori_loop(0, depth, body, 0)

    def table_step(stage, axis, src):
        table_in[stage][here[axis]] = src[...]
        return [
            send(count, src, table_in[stage].at[here[axis]], moved(here, axis, s, dims))
            for s in range(1, dims[axis])
        ]

    def table_add(stage, axis, copies, dst):
        for copy in copies:
            copy.wait_recv()
        total = table_in[stage][0]
        for j in range(1, dims[axis]):
            total = total + table_in[stage][j]
        dst[...] = total

    other = moved(here, 2, 1, dims)
    table_copies = table_step(0, 2, table)
    core_copies = []
    for k in range(count):
        axis = k % 2
        cross = 1 - axis
        group = {}
        for lag in list(range(1, dims[axis])) + [0]:
            for j in range(dims[cross]):
                at = moved(here, axis, lag, dims)
                at[cross] = j
                group[lag, j] = send(
                    k, ins[k].at[at[0], at[1], other[2]], bufs[k][0].at[at[0], at[1]], other
                )
        core_copies.append(group)
    table_add(0, 2, table_copies, table_sum[0])
    table_copies = table_step(1, 0, table_sum[0])
    first = []
    for k in range(count):
        axis = k % 2
        cross = 1 - axis
        from_core, sum_core, from_first = bufs[k][0], bufs[k][1], bufs[k][2]
        group = []
        for lag in list(range(1, dims[axis])) + [0]:
            for j in range(dims[cross]):
                at = moved(here, axis, lag, dims)
                at[cross] = j
                core_copies[k][lag, j].wait_recv()
                block = sum_core.at[at[0], at[1]]
                add(block, [ins[k].at[at[0], at[1], core], from_core.at[at[0], at[1]]])
                if lag:
                    group.append(
                        send(k, block, from_first.at[lag - 1, j], moved(here, axis, lag, dims))
                    )
        first.append(group)
    table_add(1, 0, table_copies, table_sum[1])
    table_copies = table_step(2, 1, table_sum[1])
    second = []
    for k in range(count):
        axis = k % 2
        cross = 1 - axis
        sum_core, from_first, sum_first, from_second = bufs[k][1:5]
        for copy in first[k]:
            copy.wait_recv()
        group = []
        for lag in list(range(1, dims[cross])) + [0]:
            at = moved(here, cross, lag, dims)
            j = at[cross]
            block = sum_first.at[j]
            add(
                block,
                [sum_core.at[at[0], at[1]]]
                + [from_first.at[s - 1, j] for s in range(1, dims[axis])],
            )
            if lag:
                group.append(send(k, block, from_second.at[lag - 1], at))
        second.append(group)
    table_add(2, 1, table_copies, table_sum[2])
    table_copies = table_step(3, 3, table_sum[2])
    third = []
    for k in range(count):
        axis = k % 2
        cross = 1 - axis
        sum_first, from_second, sum_second, from_third = bufs[k][3:7]
        for copy in second[k]:
            copy.wait_recv()
        add(
            sum_second,
            [sum_first.at[here[cross]]] + [from_second.at[s - 1] for s in range(1, dims[cross])],
        )
        group = []
        for step in range(1, depth):
            at = moved(here, 3, step, dims)
            group.append(send(k, sum_second.at[at[3]], from_third.at[step - 1], at))
        third.append(group)
    table_add(3, 3, table_copies, table_out)
    for k in range(count):
        sum_second, from_third = bufs[k][5:7]
        for copy in third[k]:
            copy.wait_recv()
        total = sum_second[z].astype(jnp.float32)
        for step in range(1, depth):
            total = total + from_third[step - 1].astype(jnp.float32)
        outs[k][...] = total
    for copy in started:
        copy.wait_send()


def sizes_here():
    rows, depth = lax.axis_size("rows"), lax.axis_size("cols")
    height, width = grid_of(rows)
    return height, width, CORES, depth


def blocked(rows, columns):
    if rows % 16 == 0:
        return rows, columns
    return rows * columns // 128, 128


def gather_all(shards):
    dims = sizes_here()
    height, width, cores, depth = dims
    count = len(shards)
    blocks = [blocked(*shard.shape) for shard in shards]
    slots = (depth - 1) + max(height, width) * 2 * height * width
    outs = pl.pallas_call(
        functools.partial(gather_kernel, dims, count),
        name="gather_all",
        out_shape=[
            jax.ShapeDtypeStruct(dims + block, shard.dtype)
            for block, shard in zip(blocks, shards)
        ],
        in_specs=[pl.BlockSpec(memory_space=pltpu.VMEM)] * count,
        out_specs=[pl.BlockSpec(memory_space=pl.ANY)] * count,
        scratch_shapes=[
            pltpu.SemaphoreType.DMA((count,)),
            pltpu.SemaphoreType.DMA((count, slots)),
            pltpu.SemaphoreType.DMA((count, slots)),
        ],
        compiler_params=pltpu.CompilerParams(collective_id=0, has_side_effects=True),
        cost_estimate=pl.CostEstimate(flops=0, bytes_accessed=150_000_000, transcendentals=0),
    )(*[shard.reshape(block) for block, shard in zip(blocks, shards)])
    total = height * width * cores * depth
    return [
        out.reshape(total * shard.shape[0], shard.shape[1]) for out, shard in zip(outs, shards)
    ]


def reduce_all(wholes, table):
    dims = sizes_here()
    height, width, cores, depth = dims
    total = height * width * cores * depth
    count = len(wholes)
    shares = [(whole.shape[0] // total, whole.shape[1]) for whole in wholes]
    blocks = [blocked(*share) for share in shares]
    scratch = []
    for k, (block, whole) in enumerate(zip(blocks, wholes)):
        along, cross = dims[k % 2], dims[1 - k % 2]
        for lead in (
            (height, width, depth),
            (height, width, depth),
            (max(along - 1, 1), cross, depth),
            (cross, depth),
            (max(cross - 1, 1), depth),
            (depth,),
            (max(depth - 1, 1),),
        ):
            scratch.append(pltpu.VMEM(lead + block, whole.dtype))
    for size in (cores, height, width, depth):
        scratch.append(pltpu.VMEM((size,) + table.shape, table.dtype))
    scratch += [pltpu.VMEM(table.shape, table.dtype)] * 3
    slots = 2 * height * width + height + width + depth
    scratch += [pltpu.SemaphoreType.DMA((count + 1, slots))] * 2
    outs = pl.pallas_call(
        functools.partial(reduce_kernel, dims, count),
        name="reduce_all",
        out_shape=[jax.ShapeDtypeStruct(block, jnp.float32) for block in blocks]
        + [jax.ShapeDtypeStruct(table.shape, table.dtype)],
        in_specs=[pl.BlockSpec(memory_space=pltpu.VMEM)] * (count + 1),
        out_specs=[pl.BlockSpec(memory_space=pltpu.VMEM)] * (count + 1),
        scratch_shapes=scratch,
        compiler_params=pltpu.CompilerParams(collective_id=1, has_side_effects=True),
        cost_estimate=pl.CostEstimate(flops=0, bytes_accessed=150_000_000, transcendentals=0),
    )(*[whole.reshape(dims + block) for block, whole in zip(blocks, wholes)], table)
    return [out.reshape(share) for out, share in zip(outs, shares)], outs[-1]


def padded(values, multiple):
    size = values.shape[-1]
    extra = -size % multiple
    return jnp.pad(values, [(0, 0)] * (values.ndim - 1) + [(0, extra)])


def joined(parts):
    size = sum(part.shape[0] for part in parts)
    size += -size % 2048
    total, offset = None, 0
    for part in parts:
        after = size - offset - part.shape[0]
        placed = lax.pad(part.astype(jnp.float32), jnp.float32(0), [(offset, after, 0)])
        total = placed if total is None else total + placed
        offset += part.shape[0]
    return total


def per_device(
    images,
    cotangent,
    rel_index,
    rel_table,
    qkv_weight,
    proj_weight,
    up_weight,
    down_weight,
    norm1_gain,
    norm1_bias,
    query_bias,
    value_bias,
    proj_bias,
    norm2_gain,
    norm2_bias,
    up_bias,
    down_bias,
):
    shards = (
        norm1_gain,
        norm1_bias,
        query_bias,
        value_bias,
        proj_bias,
        norm2_gain,
        norm2_bias,
        up_bias,
        down_bias,
    )
    vector_shard = joined(shards).astype(jnp.bfloat16).reshape(-1, 128)
    qkv_full, down_full, up_full, proj_full, vector_full = gather_all(
        [qkv_weight, down_weight, up_weight, proj_weight, vector_shard]
    )
    device_count = lax.axis_size("rows") * lax.axis_size("cols")
    vector_full = vector_full.reshape(device_count, -1)
    vectors, offset = [], 0
    for shard in shards:
        size = shard.shape[0]
        vectors.append(vector_full[:, offset : offset + size].reshape(device_count * size))
        offset += size
    (
        gain_one_full,
        bias_one_full,
        query_add,
        value_add,
        proj_add,
        gain_two_full,
        bias_two_full,
        up_add,
        down_add,
    ) = vectors
    tokens_tile, grad_tile = roll_in(images), roll_in(cotangent)
    image_count, tile_side, features = (
        tokens_tile.shape[0],
        tokens_tile.shape[1],
        tokens_tile.shape[3],
    )
    window = tile_side * tile_side
    row_total = image_count * window
    tokens = tokens_tile.reshape(row_total, features)
    grad_rows = grad_tile.reshape(row_total, features)
    local_pos = jnp.arange(tile_side, dtype=jnp.int32)
    band_rows = band_of(
        lax.axis_index("rows") * tile_side + local_pos, lax.axis_size("rows") * tile_side
    )
    band_cols = band_of(
        lax.axis_index("cols") * tile_side + local_pos, lax.axis_size("cols") * tile_side
    )
    region = (3 * band_rows[:, None] + band_cols[None, :]).reshape(window)
    allowed = (region[:, None] == region[None, :])[None, None]
    head_count = rel_table.shape[1]
    table_size = rel_table.shape[0]
    head_width = features // head_count
    score_scale = head_width ** (-0.5)
    onehot = (
        rel_index.reshape(window * window)[:, None]
        == jnp.arange(table_size, dtype=jnp.int32)[None, :]
    ).astype(jnp.float32)
    bias_flat = jnp.dot(
        onehot, rel_table, precision=lax.Precision.HIGHEST, preferred_element_type=jnp.float32
    )
    bias_heads = bias_flat.T.reshape(head_count, window, window)

    def split_heads(values):
        return values.reshape(image_count, window, head_count, head_width)

    def scores_of(query_b, key_b):
        raw_scores = jnp.einsum(
            "wqhd,wkhd->whqk",
            split_heads(query_b),
            split_heads(key_b),
            preferred_element_type=jnp.float32,
        )
        return jnp.where(allowed, raw_scores + bias_heads[None], big_negative)

    gain_one = gain_one_full.astype(jnp.float32)
    gain_two = gain_two_full.astype(jnp.float32)
    out_one, normed_one, inv_one = layer_norm(tokens, gain_one, bias_one_full.astype(jnp.float32))
    h_one = out_one.astype(jnp.bfloat16)
    projected = dot_plain(h_one, qkv_full)
    query_b = ((projected[:, :features] + query_add.astype(jnp.float32)) * score_scale).astype(
        jnp.bfloat16
    )
    key_b = projected[:, features : 2 * features].astype(jnp.bfloat16)
    value_b = (projected[:, 2 * features :] + value_add.astype(jnp.float32)).astype(jnp.bfloat16)
    scores = scores_of(query_b, key_b)
    row_top = jnp.max(scores, axis=-1, keepdims=True)
    log_total = row_top + jnp.log(jnp.sum(jnp.exp(scores - row_top), axis=-1, keepdims=True))
    attend_b = jnp.exp(scores - log_total).astype(jnp.bfloat16)
    attn_b = (
        jnp.einsum(
            "whqk,wkhd->wqhd", attend_b, split_heads(value_b), preferred_element_type=jnp.float32
        )
        .reshape(row_total, features)
        .astype(jnp.bfloat16)
    )
    residual = tokens + dot_plain(attn_b, proj_full) + proj_add.astype(jnp.float32)
    out_two, normed_two, inv_two = layer_norm(residual, gain_two, bias_two_full.astype(jnp.float32))
    h_two = out_two.astype(jnp.bfloat16)
    hidden_pre = dot_plain(h_two, up_full) + up_add.astype(jnp.float32)
    gauss_cdf = 0.5 * (1.0 + lax.erf(hidden_pre * root_half))
    act_b = (hidden_pre * gauss_cdf).astype(jnp.bfloat16)
    result = residual + dot_plain(act_b, down_full) + down_add.astype(jnp.float32)
    grad_b = grad_rows.astype(jnp.bfloat16)
    grad_down = dot_lead(act_b, grad_b)
    grad_down_add = jnp.sum(grad_rows, axis=0)
    grad_act = dot_tail(grad_b, down_full)
    density = jnp.exp(-0.5 * hidden_pre * hidden_pre) * tau_factor
    grad_pre = grad_act * (gauss_cdf + hidden_pre * density)
    grad_pre_b = grad_pre.astype(jnp.bfloat16)
    grad_up = dot_lead(h_two, grad_pre_b)
    grad_up_add = jnp.sum(grad_pre, axis=0)
    grad_h_two = dot_tail(grad_pre_b, up_full)
    grad_resid, grad_gain_two, grad_bias_two = norm_back(
        grad_h_two, normed_two, inv_two, gain_two
    )
    grad_resid = grad_resid + grad_rows
    grad_resid_b = grad_resid.astype(jnp.bfloat16)
    grad_proj = dot_lead(attn_b, grad_resid_b)
    grad_proj_add = jnp.sum(grad_resid, axis=0)
    grad_attn_b = dot_tail(grad_resid_b, proj_full).astype(jnp.bfloat16)
    grad_heads = split_heads(grad_attn_b)
    grad_attend = jnp.einsum(
        "wqhd,wkhd->whqk", grad_heads, split_heads(value_b), preferred_element_type=jnp.float32
    )
    attend = jnp.exp(scores_of(query_b, key_b) - log_total)
    grad_value = jnp.einsum(
        "whqk,wqhd->wkhd",
        attend.astype(jnp.bfloat16),
        grad_heads,
        preferred_element_type=jnp.float32,
    ).reshape(row_total, features)
    row_inner = jnp.sum(attend * grad_attend, axis=-1, keepdims=True)
    grad_scores = attend * (grad_attend - row_inner)
    grad_bias_heads = jnp.sum(grad_scores, axis=0).reshape(head_count, window * window)
    table_local = lax.dot_general(
        onehot,
        grad_bias_heads,
        (((0,), (1,)), ((), ())),
        precision=lax.Precision.HIGHEST,
        preferred_element_type=jnp.float32,
    )
    grad_scores_b = grad_scores.astype(jnp.bfloat16)
    grad_query = (
        jnp.einsum(
            "whqk,wkhd->wqhd", grad_scores_b, split_heads(key_b), preferred_element_type=jnp.float32
        )
        * score_scale
    ).reshape(row_total, features)
    grad_key = jnp.einsum(
        "whqk,wqhd->wkhd", grad_scores_b, split_heads(query_b), preferred_element_type=jnp.float32
    ).reshape(row_total, features)
    grad_query_add = jnp.sum(grad_query, axis=0)
    grad_value_add = jnp.sum(grad_value, axis=0)
    grad_mixed_b = jnp.concatenate([grad_query, grad_key, grad_value], axis=1).astype(jnp.bfloat16)
    grad_qkv = dot_lead(h_one, grad_mixed_b)
    grad_h_one = dot_tail(grad_mixed_b, qkv_full)
    grad_in, grad_gain_one, grad_bias_one = norm_back(
        grad_h_one, normed_one, inv_one, gain_one
    )
    grad_tokens = grad_resid + grad_in
    vector_grads = (
        grad_gain_one,
        grad_bias_one,
        grad_query_add,
        grad_value_add,
        grad_proj_add,
        grad_gain_two,
        grad_bias_two,
        grad_up_add,
        grad_down_add,
    )
    vector_rows = padded(
        jnp.concatenate([grad.reshape(device_count, -1) for grad in vector_grads], axis=1), 2048
    ).reshape(-1, 128)
    block_out = roll_out(result.reshape(image_count, tile_side, tile_side, features))
    grad_tokens, table_local = lax.optimization_barrier((grad_tokens, table_local))
    grad_images = roll_out(grad_tokens.reshape(image_count, tile_side, tile_side, features))
    table_rows = padded(table_local.reshape(1, -1), 1024).reshape(-1, 128)
    (down_sum, up_sum, qkv_sum, proj_sum, vector_sum), table_sum = reduce_all(
        [
            grad_down.astype(jnp.bfloat16),
            grad_up.astype(jnp.bfloat16),
            grad_qkv.astype(jnp.bfloat16),
            grad_proj.astype(jnp.bfloat16),
            vector_rows,
        ],
        table_rows,
    )
    grad_table = table_sum.reshape(-1)[: table_local.size].reshape(table_local.shape)
    vector_sum = vector_sum.reshape(-1)
    vector_sums, offset = [], 0
    for shard in shards:
        size = shard.shape[0]
        vector_sums.append(vector_sum[offset : offset + size])
        offset += size
    shard_grads = (qkv_sum, proj_sum, up_sum, down_sum, *vector_sums)
    return (
        block_out,
        grad_images,
        shard_grads[0],
        shard_grads[1],
        shard_grads[2],
        shard_grads[3],
        shard_grads[4],
        shard_grads[5],
        shard_grads[6],
        shard_grads[7],
        shard_grads[8],
        shard_grads[9],
        shard_grads[10],
        shard_grads[11],
        shard_grads[12],
        grad_table,
    )


def solution(mesh):
    in_specs = (
        P(None, "rows", "cols", None),
        P(None, "rows", "cols", None),
        P(),
        P(),
        P(("rows", "cols"), None),
        P(("rows", "cols"), None),
        P(("rows", "cols"), None),
        P(("rows", "cols"), None),
        P(("rows", "cols")),
        P(("rows", "cols")),
        P(("rows", "cols")),
        P(("rows", "cols")),
        P(("rows", "cols")),
        P(("rows", "cols")),
        P(("rows", "cols")),
        P(("rows", "cols")),
        P(("rows", "cols")),
    )
    out_specs = (
        P(None, "rows", "cols", None),
        P(None, "rows", "cols", None),
        P(("rows", "cols"), None),
        P(("rows", "cols"), None),
        P(("rows", "cols"), None),
        P(("rows", "cols"), None),
        P(("rows", "cols")),
        P(("rows", "cols")),
        P(("rows", "cols")),
        P(("rows", "cols")),
        P(("rows", "cols")),
        P(("rows", "cols")),
        P(("rows", "cols")),
        P(("rows", "cols")),
        P(("rows", "cols")),
        P(),
    )
    return jax.shard_map(
        per_device, mesh=mesh, in_specs=in_specs, out_specs=out_specs, check_vma=False
    )
```
